32 devices in a mesh: seq: 8 (over z, x), head: 4 (over y, core).
Axes of the slice: x: 2, y: 2, z: 4, core: 2. Of those that a mesh axis runs over, the one named last changes fastest.
Arguments:
- queries: bfloat16 [3072, 2048], P('seq', 'head'), may hold values from -120 to 120
- keys: bfloat16 [3072, 2048], P('seq', 'head'), may hold values from -5 to 5
- values: bfloat16 [3072, 2048], P('seq', 'head'), may hold values from -5 to 5
- directions: bfloat16 [3072, 2048], P('seq', 'head'), may hold values from -5 to 5
- beta_logit: float32 [16, 3072], P('head', 'seq'), may hold values from -3 to 7
- out_weight: bfloat16 [2048, 2048], P('head'), may hold values from -0.1875 to 0.1875
Outputs:
- mixed: bfloat16 [3072, 2048], P('seq', 'head')
The draws below stay inside these ranges and needn't reach their ends.
All inputs are finite; a program needn't handle non-finite values.
Results may differ from the reference program's by a relative error of at most 0.015.
Values may be sent and summed in bfloat16 or wider, within the bound.
No kernel may reach another device: no remote copies, remote signals or barrier semaphores. Data moves between devices by JAX's collectives and lax.ppermute only.
A program may use at most 64 MiB of HBM per device.

```python
import math
import jax
import jax.numpy as jnp
from jax import lax

HEADS = 16
HEAD_DIM = 128
D = 2048
SUB = 128
WINDOW = 4
TOK_DEV = 384
TOKENS = 3072
N_SEQ = 8


def drawn_rows(key):
    width = HEADS * HEAD_DIM
    base_keys = jnp.clip(jax.random.normal(jax.random.fold_in(key, 11), (TOKENS, width), jnp.float32), -4.5, 4.5)
    base_queries = jnp.clip(jax.random.normal(jax.random.fold_in(key, 12), (TOKENS, width), jnp.float32), -4.5, 4.5)
    return (base_queries, base_keys)


def draw_queries(key, part):
    queries_out, keys_out = drawn_rows(key)
    return queries_out.astype(jnp.bfloat16)


def draw_keys(key, part):
    queries_out, keys_out = drawn_rows(key)
    return keys_out.astype(jnp.bfloat16)


def draw_beta_logit(key, part):
    shape_all = (HEADS, TOKENS)
    strong = jax.random.uniform(jax.random.fold_in(key, 21), shape_all, jnp.float32, 3.5, 7.0)
    softer = jax.random.uniform(jax.random.fold_in(key, 22), shape_all, jnp.float32, -3.0, 1.0)
    rarely = jax.random.bernoulli(jax.random.fold_in(key, 23), 1.0 / 64.0, shape_all)
    return jnp.where(rarely, softer, strong).astype(jnp.float32)


def with_spikes(drawn, key, source, target, shards_of, factor):
    owner, partner = [(jnp.arange(drawn.shape[axis_at]) // (drawn.shape[axis_at] // shards_of)).reshape([-1 if axis == axis_at else 1 for axis in range(drawn.ndim)]) for axis_at in (source, target)]
    chosen = jax.random.permutation(key, shards_of)[partner]
    strong = (owner == chosen) | (owner == (partner + shards_of // 2) % shards_of)
    return jnp.where(strong, factor * drawn, drawn)


def level_of(key, dims, pieces, smallest, top_value):
    level, own = 1.0, jax.random.fold_in(key, 6)
    for dim, blocks in pieces:
        steps = jnp.exp(jax.random.uniform(jax.random.fold_in(own, dim), (blocks,), jnp.float32, smallest / len(pieces), top_value / len(pieces)))
        level = level * jnp.repeat(steps, dims[dim] // blocks).reshape([-1 if axis == dim else 1 for axis in range(len(dims))])
    return level


def bell_draw(stream_key, extent, scale, bound, cuts=(), held_as=jnp.bfloat16):
    level = level_of(stream_key, extent, cuts, -0.22, 0.18) if cuts else 1.0
    drawn = jax.random.normal(stream_key, extent, jnp.float32) * scale * level
    return jnp.minimum(jnp.maximum(drawn, -bound), bound).astype(held_as)


def bell_draw_with(key, shape, scale, reach, pieces, heavy, held_as=jnp.bfloat16):
    values = scale * jax.random.normal(key, shape, jnp.float32)
    if pieces:
        values = values * level_of(key, shape, pieces, -0.22, 0.18)
    return jnp.clip(with_spikes(values, jax.random.fold_in(key, 3), *heavy), -reach, reach).astype(held_as)


def setup_inputs(seed: int = 0) -> dict:
    key_list = jax.random.split(jax.random.key(seed), 7)
    return {
        "queries": draw_queries(jax.random.fold_in(key_list[6], 71), 0),
        "keys": draw_keys(jax.random.fold_in(key_list[6], 71), 0),
        "values": bell_draw(key_list[2], (TOKENS, HEADS * HEAD_DIM), 1.0, 5.0, ((0, 8), (1, 4))),
        "directions": bell_draw(key_list[3], (TOKENS, HEADS * HEAD_DIM), 1.0, 5.0, ((0, 8), (1, 4))),
        "beta_logit": draw_beta_logit(jax.random.fold_in(key_list[6], 71), 0),
        "out_weight": bell_draw_with(key_list[5], (HEADS * HEAD_DIM, D), (HEADS * HEAD_DIM) ** -0.5, 0.1875, ((0, 4),), (0, 1, 4, 2.0)),
    }


highest = lax.Precision.HIGHEST

def product(pattern, first_op, second_op):
    return jnp.einsum(pattern, first_op, second_op, precision=highest)

def solve_unit(matrix):
    identity_run = jnp.eye(matrix.shape[0], dtype=matrix.dtype)
    return jax.scipy.linalg.solve_triangular(matrix, identity_run, lower=True, unit_diagonal=True)

def block_local(query_rows, key_rows, direction_rows, logits, run_size):
    head_count, length, head_size = query_rows.shape
    run_count = length // run_size
    shape_runs = (head_count, run_count, run_size, head_size)
    queries32 = query_rows.astype(jnp.float32).reshape(shape_runs)
    keys32 = key_rows.astype(jnp.float32).reshape(shape_runs)
    raw_dirs = direction_rows.astype(jnp.float32)
    unit_dirs = (raw_dirs * lax.rsqrt(lax.optimization_barrier(jnp.sum(raw_dirs * raw_dirs, axis=-1, keepdims=True)) + 1e-06)).reshape(shape_runs)
    betas = (2.0 * jax.nn.sigmoid(logits.astype(jnp.float32))).reshape(head_count, run_count, run_size)
    ones_run = jnp.ones((run_size, run_size), jnp.float32)
    strict_lower = jnp.tril(ones_run, -1)
    inclusive = jnp.tril(ones_run, 0)
    strict_upper = jnp.triu(ones_run, 1)
    identity_run = jnp.eye(run_size, dtype=jnp.float32)
    grams = product('hnce,hnde->hncd', unit_dirs, unit_dirs)
    system = identity_run + grams * strict_lower * betas[:, :, None, :]
    inverse = jax.vmap(solve_unit)(system.reshape(-1, run_size, run_size)).reshape(system.shape)
    coeffs = betas[:, :, :, None] * inverse
    coeff_dirs = product('hnac,hncd->hnad', coeffs, unit_dirs)
    coeff_back = product('hnca,hncd->hnad', coeffs, unit_dirs)
    identity_head = jnp.eye(head_size, dtype=jnp.float32)
    run_maps = identity_head - product('hncd,hnce->hnde', unit_dirs, coeff_dirs)
    query_dirs = product('hnid,hnad->hnia', queries32, unit_dirs) * inclusive
    query_start = queries32 - product('hnia,hnad->hnid', query_dirs, coeff_dirs)
    key_dirs = product('hnjd,hncd->hnjc', keys32, unit_dirs) * strict_upper
    key_end = keys32 - product('hnjc,hncd->hnjd', key_dirs, coeff_back)
    mixed_dirs = product('hnac,hnjc->hnaj', coeffs, key_dirs)
    inside = product('hnid,hnjd->hnij', queries32, keys32) - product('hnia,hnaj->hnij', query_dirs, mixed_dirs)
    inside = jnp.where(inclusive > 0, inside, -jnp.inf)
    carried = jnp.zeros((head_count, length, head_size), jnp.float32)
    prefix = jnp.broadcast_to(identity_head, (head_count, head_size, head_size))
    row_parts = []
    query_parts = []
    for index_run in range(run_count):
        starts = query_start[:, index_run]
        query_parts.append(product('hid,hde->hie', starts, prefix))
        across = product('hid,hjd->hij', starts, carried)
        before = index_run * run_size
        after = length - before - run_size
        filler = jnp.full((head_count, run_size, after), -jnp.inf, jnp.float32)
        row_parts.append(jnp.concatenate([across[:, :, :before], inside[:, index_run], filler], axis=2))
        carried = product('hjd,hed->hje', carried, run_maps[:, index_run])
        carried = lax.dynamic_update_slice_in_dim(carried, key_end[:, index_run], before, 1)
        prefix = product('hde,hef->hdf', run_maps[:, index_run], prefix)
    own_scores = jnp.concatenate(row_parts, axis=1)
    query_block = jnp.concatenate(query_parts, axis=1)
    return (own_scores, query_block, carried, prefix)

def attend(score_parts, value_parts, head_size):
    scores = jnp.concatenate(score_parts, axis=2) * (1.0 / math.sqrt(head_size))
    maxima = lax.optimization_barrier(jnp.max(scores, axis=2, keepdims=True))
    weights = jnp.exp(scores - maxima)
    totals = lax.optimization_barrier(jnp.sum(weights, axis=2, keepdims=True))
    rounded = weights.astype(jnp.bfloat16)
    values_all = jnp.concatenate(value_parts, axis=1)
    attended = jnp.einsum('hik,hkd->hid', rounded.astype(jnp.float32), values_all.astype(jnp.float32), precision=highest)
    return (attended / totals).astype(jnp.bfloat16)

def reference(queries, keys, values, directions, beta_logit, out_weight):

    def blocks(array):
        return array.reshape(N_SEQ, TOK_DEV, HEADS, HEAD_DIM).transpose(0, 2, 1, 3)
    query_all = blocks(queries)
    key_all = blocks(keys)
    value_all = blocks(values)
    dir_all = blocks(directions)
    logit_all = beta_logit.reshape(HEADS, N_SEQ, TOK_DEV).transpose(1, 0, 2)

    def pick(array, index_block):
        return lax.dynamic_index_in_dim(array, index_block, 0, keepdims=False)

    def local_pass(index_block):
        result = block_local(pick(query_all, index_block), pick(key_all, index_block), pick(dir_all, index_block), pick(logit_all, index_block), SUB)
        return (result[1], result[2], result[3])
    block_ids = jnp.arange(N_SEQ, dtype=jnp.int32)
    query_tilde, key_tilde, block_maps = lax.map(local_pass, block_ids)
    key_rounded = key_tilde.astype(jnp.bfloat16)
    identity_head = jnp.eye(HEAD_DIM, dtype=jnp.float32)

    def window_pass(index_block):
        own_scores, query_block, unused_keys, unused_map = block_local(pick(query_all, index_block), pick(key_all, index_block), pick(dir_all, index_block), pick(logit_all, index_block), SUB)
        score_parts = [own_scores]
        value_parts = [pick(value_all, index_block)]
        composed = jnp.broadcast_to(identity_head, (HEADS, HEAD_DIM, HEAD_DIM))
        for distance in range(1, WINDOW + 1):
            source = jnp.maximum(index_block - distance, 0).astype(jnp.int32)
            if distance > 1:
                middle = jnp.maximum(index_block - distance + 1, 0).astype(jnp.int32)
                composed = product('hde,hef->hdf', composed, pick(block_maps, middle))
            moved = product('hjd,hed->hje', pick(key_rounded, source).astype(jnp.float32), composed)
            remote = product('hid,hjd->hij', query_block, moved)
            score_parts.append(jnp.where(index_block >= distance, remote, -jnp.inf))
            value_parts.append(pick(value_all, source))
        return attend(score_parts, value_parts, HEAD_DIM)
    outputs = lax.map(window_pass, block_ids)
    attn = outputs.transpose(0, 2, 1, 3).reshape(TOKENS, HEADS * HEAD_DIM)
    return jnp.dot(attn.astype(jnp.float32), out_weight.astype(jnp.float32), preferred_element_type=jnp.float32).astype(jnp.bfloat16)
```

```python
import functools
import math

import jax
import jax.numpy as jnp
from jax import lax
from jax.experimental import pallas as pl
from jax.experimental.pallas import tpu as pltpu
from jax.sharding import PartitionSpec as P

SUB = 128
WINDOW = 4
F32 = jnp.float32
BF16 = jnp.bfloat16
MIB = 1 << 20


def split(x):
    high = x.astype(BF16)
    return high, (x - high.astype(F32)).astype(BF16)


def mm(a, b):
    return lax.dot_general(a, b, (((1,), (0,)), ((), ())), preferred_element_type=F32)


def mm_nt(a, b):
    return lax.dot_general(a, b, (((1,), (1,)), ((), ())), preferred_element_type=F32)


def mm_tn(a, b):
    return lax.dot_general(a, b, (((0,), (0,)), ((), ())), preferred_element_type=F32)


def dot3(a, b):
    (ah, al), (bh, bl) = split(a), split(b)
    return mm(jnp.concatenate([ah, al, ah], 1), jnp.concatenate([bh, bh, bl], 0))


def dot3_nt(a, b):
    (ah, al), (bh, bl) = split(a), split(b)
    return mm_nt(jnp.concatenate([ah, al, ah], 1), jnp.concatenate([bh, bh, bl], 1))


def dot2(a, b):
    ah, al = split(a)
    return mm(jnp.concatenate([ah, al], 1), jnp.concatenate([b, b], 0))


def iotas(size):
    rows = lax.broadcasted_iota(jnp.int32, (size, size), 0)
    cols = lax.broadcasted_iota(jnp.int32, (size, size), 1)
    return rows, cols


def local_kernel(heads, first, runs, k_ref, w_ref, logit_ref, kp_ref, coef_ref, mixed_ref, end_ref, map_ref, low, inv, gamma):
    size = k_ref.shape[1] // heads
    length = runs * SUB
    rows, cols = iotas(SUB)
    eye = (rows == cols).astype(F32)
    units = [(h, r) for h in range(heads) for r in range(runs)]

    def at(ref, h, r):
        return ref[r * SUB : (r + 1) * SUB, h * size : (h + 1) * size]

    for u, (h, r) in enumerate(units):
        w = at(w_ref, h, r)
        gram = mm_nt(w, w)
        norm = jnp.sum(gram * eye, axis=0, keepdims=True)
        logit = logit_ref[first + h : first + h + 1, r * SUB : (r + 1) * SUB]
        strength = 2.0 * jax.nn.sigmoid(logit) / (norm + 1e-06)
        gamma[u] = jnp.broadcast_to(strength, (8, SUB))
        lower = jnp.where(rows > cols, gram * strength, 0.0)
        low[u] = lower
        pair = (rows // 2 == cols // 2)
        inv[u] = eye - jnp.where(pair, lower, 0.0)
    block = 2
    while block < SUB:
        mask = (rows // (2 * block) == cols // (2 * block)) & (rows // block != cols // block)
        for u in range(len(units)):
            x = inv[u]
            step = dot3(x, jnp.where(mask, low[u], 0.0))
            inv[u] = x - dot3(step, x)
        block *= 2
    for u, (h, r) in enumerate(units):
        w = at(w_ref, h, r)
        k = at(k_ref, h, r)
        x = inv[u]
        strength = gamma[u][0:1]
        column = jnp.sum(eye * strength, axis=1, keepdims=True)
        coef = dot2(x, w) * column
        coef_ref[r * SUB : (r + 1) * SUB, h * size : (h + 1) * size] = coef
        ch, cl = split(coef)
        run_map = jnp.where(rows == cols, 1.0, 0.0) - mm_tn(jnp.concatenate([w, w], 0), jnp.concatenate([ch, cl], 0))
        key_dirs = jnp.where(cols > rows, mm_nt(k, w), 0.0)
        mixed = dot3_nt(key_dirs, x) * strength
        mixed_ref[r * SUB : (r + 1) * SUB, h * size : (h + 1) * size] = mixed
        end_ref[r * SUB : (r + 1) * SUB, h * size : (h + 1) * size] = k.astype(F32) - dot2(mixed, w)
        map_ref[r * SUB : (r + 1) * SUB, h * size : (h + 1) * size] = run_map
    for h in range(heads):
        span = slice(h * size, (h + 1) * size)
        after = None
        for r in reversed(range(runs)):
            ends = at(end_ref, h, r)
            run_map = at(map_ref, h, r)
            moved = ends if after is None else dot3_nt(ends, after)
            kp_ref[r * SUB : (r + 1) * SUB, span] = moved.astype(BF16)
            after = run_map if after is None else dot3(after, run_map)
        ph, plow = split(after)
        kp_ref[length : length + size, span] = ph
        kp_ref[length + size : length + 2 * size, span] = plow


def local_keys(keys, directions, logits, heads, first):
    length, width = keys.shape
    size = width // logits.shape[0]
    runs = length // SUB
    chunk = first // heads
    part = pl.BlockSpec((length, heads * size), lambda i: (0, chunk))
    whole = jax.ShapeDtypeStruct((length, heads * size), F32)
    units = heads * runs
    return pl.pallas_call(
        functools.partial(local_kernel, heads, first, runs),
        grid=(1,),
        in_specs=[part, part, pl.BlockSpec(logits.shape, lambda i: (0, 0))],
        out_specs=[pl.BlockSpec((length + 2 * size, heads * size), lambda i: (0, 0))]
        + [pl.BlockSpec((length, heads * size), lambda i: (0, 0))] * 4,
        out_shape=[jax.ShapeDtypeStruct((length + 2 * size, heads * size), BF16), whole, whole, whole, whole],
        scratch_shapes=[
            pltpu.VMEM((units, SUB, SUB), F32),
            pltpu.VMEM((units, SUB, SUB), F32),
            pltpu.VMEM((units, 8, SUB), F32),
        ],
        compiler_params=pltpu.CompilerParams(vmem_limit_bytes=24 * MIB),
        cost_estimate=pl.CostEstimate(
            flops=units * 60 * 2 * SUB**3 * 8, bytes_accessed=units * SUB * SUB * 24, transcendentals=0
        ),
        name="local_keys",
    )(keys, directions, logits)


def pack_stats(maxima, totals):
    lanes = lax.broadcasted_iota(jnp.int32, (maxima[0].shape[0], 128), 1)
    out = jnp.zeros(lanes.shape, F32)
    for i, column in enumerate(list(maxima) + list(totals)):
        out = jnp.where(lanes == i, column, out)
    return out


def own_kernel(heads, runs, q_ref, k_ref, w_ref, v_ref, coef_ref, mixed_ref, end_ref, map_ref, qt_ref, acc_ref, stat_ref):
    size = q_ref.shape[1] // heads
    rows, cols = iotas(SUB)
    scale = 1.0 / math.sqrt(size)

    def at(ref, h, r):
        return ref[r * SUB : (r + 1) * SUB, h * size : (h + 1) * size]

    for r in range(runs):
        here = slice(r * SUB, (r + 1) * SUB)
        maxima, totals = [], []
        for h in range(heads):
            span = slice(h * size, (h + 1) * size)
            q, k, w = at(q_ref, h, r), at(k_ref, h, r), at(w_ref, h, r)
            dirs = jnp.where(cols <= rows, mm_nt(q, w), 0.0)
            start = q.astype(F32) - dot3(dirs, at(coef_ref, h, r))
            inside = mm_nt(q, k) - dot3_nt(dirs, at(mixed_ref, h, r))
            parts = [jnp.where(cols <= rows, inside * scale, -jnp.inf)]
            for other in reversed(range(r)):
                parts.insert(0, dot3_nt(start, at(end_ref, h, other)) * scale)
                start = dot3(start, at(map_ref, h, other))
            qt_ref[here, span] = start
            scores = jnp.concatenate(parts, 1)
            top = jnp.max(scores, axis=1, keepdims=True)
            weights = jnp.exp(scores - top)
            maxima.append(top)
            totals.append(jnp.sum(weights, axis=1, keepdims=True))
            acc_ref[here, span] = mm(weights.astype(BF16), v_ref[: (r + 1) * SUB, span])
        stat_ref[here, :] = pack_stats(maxima, totals)


def own_block(queries, keys, directions, values, aux, heads, first, size):
    length = queries.shape[0]
    runs = length // SUB
    chunk = first // heads
    part = pl.BlockSpec((length, heads * size), lambda i: (0, chunk))
    whole = pl.BlockSpec((length, heads * size), lambda i: (0, 0))
    units = heads * runs
    return pl.pallas_call(
        functools.partial(own_kernel, heads, runs),
        grid=(1,),
        in_specs=[part] * 4 + [whole] * 4,
        out_specs=[whole, whole, pl.BlockSpec((length, 128), lambda i: (0, 0))],
        out_shape=[jax.ShapeDtypeStruct((length, heads * size), F32)] * 2 + [jax.ShapeDtypeStruct((length, 128), F32)],
        compiler_params=pltpu.CompilerParams(vmem_limit_bytes=24 * MIB),
        cost_estimate=pl.CostEstimate(
            flops=units * 25 * 2 * SUB**3 * 8, bytes_accessed=units * SUB * SUB * 32, transcendentals=0
        ),
        name="own_block",
    )(queries, keys, directions, values, *aux)


def remote_kernel(heads, runs, distances, last, position_ref, q_ref, acc_in, stat_in, *refs):
    count = len(distances)
    blocks, vals = refs[:count], refs[count : 2 * count]
    previous = refs[2 * count]
    outs = refs[2 * count + 1 :]
    size = q_ref.shape[1] // heads
    length = runs * SUB
    scale = 1.0 / math.sqrt(size)
    position = position_ref[0]
    for r in range(runs):
        here = slice(r * SUB, (r + 1) * SUB)
        maxima, totals = [], []
        for h in range(heads):
            span = slice(h * size, (h + 1) * size)
            q = q_ref[here, span]
            parts = []
            for i, distance in enumerate(distances):
                if distance > 1:
                    source = previous if i == 0 else blocks[i - 1]
                    ph, plow = source[length : length + size, span], source[length + size : length + 2 * size, span]
                    qh, ql = split(q)
                    q = mm(jnp.concatenate([qh, ql, qh], 1), jnp.concatenate([ph, ph, plow], 0))
                qh, ql = split(q)
                kt = blocks[i][:length, span]
                found = mm_nt(jnp.concatenate([qh, ql], 1), jnp.concatenate([kt, kt], 1))
                bias = jnp.where(position >= distance, 0.0, -jnp.inf)
                parts.append(found * scale + bias)
            scores = jnp.concatenate(parts, 1)
            stat = stat_in[here, :]
            old = stat[:, h : h + 1]
            top = jnp.maximum(old, jnp.max(scores, axis=1, keepdims=True))
            fade = jnp.exp(old - top)
            weights = jnp.exp(scores - top)
            total = stat[:, heads + h : heads + h + 1] * fade + jnp.sum(weights, axis=1, keepdims=True)
            acc = acc_in[here, span] * fade
            rounded = weights.astype(BF16)
            for i in range(count):
                acc += mm(rounded[:, i * length : (i + 1) * length], vals[i][:, span])
            if last:
                outs[0][here, span] = (acc / total).astype(BF16)
            else:
                outs[0][here, span] = q
                outs[1][here, span] = acc
                maxima.append(top)
                totals.append(total)
        if not last:
            outs[2][here, :] = pack_stats(maxima, totals)


def remote_blocks(position, state, blocks, values, previous, distances, last, heads, first, size):
    q, acc, stat = state
    length = q.shape[0]
    runs = length // SUB
    chunk = first // heads
    whole = pl.BlockSpec((length, heads * size), lambda i: (0, 0))
    stats = pl.BlockSpec((length, 128), lambda i: (0, 0))
    packed = pl.BlockSpec(blocks[0].shape, lambda i: (0, 0))
    part = pl.BlockSpec((length, heads * size), lambda i: (0, chunk))
    state_shape = jax.ShapeDtypeStruct((length, heads * size), F32)
    count = len(distances)
    if last:
        out_specs, out_shape = [whole], [jax.ShapeDtypeStruct((length, heads * size), BF16)]
    else:
        out_specs = [whole, whole, stats]
        out_shape = [state_shape, state_shape, jax.ShapeDtypeStruct((length, 128), F32)]
    return pl.pallas_call(
        functools.partial(remote_kernel, heads, runs, distances, last),
        grid=(1,),
        in_specs=[pl.BlockSpec(memory_space=pltpu.SMEM), whole, whole, stats]
        + [packed] * count
        + [part] * count
        + [packed],
        out_specs=out_specs,
        out_shape=out_shape,
        compiler_params=pltpu.CompilerParams(vmem_limit_bytes=24 * MIB),
        cost_estimate=pl.CostEstimate(
            flops=heads * runs * 60 * 2 * SUB**3, bytes_accessed=length * size * heads * 24, transcendentals=0
        ),
        name="remote_blocks",
    )(position, q, acc, stat, *blocks, *values, previous)


def project_kernel(count, *refs):
    rows, weights, out = refs[:count], refs[count : 2 * count], refs[2 * count]
    rest = refs[2 * count + 1 :]
    total = mm(rows[0][...], weights[0][...])
    for i in range(1, count):
        total += mm(rows[i][...], weights[i][...])
    out[...] = total.astype(out.dtype)


def project(parts, weights):
    rows = [r for r, _ in parts]
    length = rows[0].shape[0]
    width = weights[0].shape[1]
    specs_rows = [pl.BlockSpec(r.shape, lambda i: (0, 0)) for r in rows]
    specs_weights = []
    for r, (_, at) in zip(rows, parts):
        specs_weights.append(pl.BlockSpec((r.shape[1], width), functools.partial(lambda at, i: (at, 0), at)))
    return pl.pallas_call(
        functools.partial(project_kernel, len(rows)),
        grid=(1,),
        in_specs=specs_rows + specs_weights,
        out_specs=pl.BlockSpec((length, width), lambda i: (0, 0)),
        out_shape=jax.ShapeDtypeStruct((length, width), BF16),
        compiler_params=pltpu.CompilerParams(vmem_limit_bytes=24 * MIB),
        name="project",
    )(*rows, *weights)


def ring(x, axis, distance):
    n = lax.axis_size(axis)
    return lax.ppermute(x, axis, [(i, (i + distance) % n) for i in range(n)])


def swap(x, axis, bit):
    n = lax.axis_size(axis)
    return lax.ppermute(x, axis, [(i, i ^ bit) for i in range(n)])


def neighbours(block, odd):
    two = ring(block, "seq", 2)
    four = ring(two, "seq", 2)
    one = swap(jnp.where(odd, two, block), "seq", 1)
    three = swap(jnp.where(odd, four, two), "seq", 1)
    return one, two, three, four


def per_device(queries, keys, values, directions, beta_logit, out_weight):
    length, width = queries.shape
    head_count = beta_logit.shape[0]
    size = width // head_count
    groups = lax.axis_size("head")
    heads = 2
    position = lax.axis_index("seq")
    group = lax.axis_index("head")
    odd = position % 2 == 1
    where = jnp.reshape(position, (1,)).astype(jnp.int32)

    near_values = neighbours(values, odd)
    columns = out_weight.shape[1] // groups
    weights = []
    for p in range(groups):
        piece = lax.dynamic_slice_in_dim(out_weight, (group ^ p) * columns, columns, 1)
        weights.append(piece if p == 0 else swap(piece, "head", p))

    gathered, matching = [], []
    firsts = range(0, head_count, heads)
    locals_ = [local_keys(keys, directions, beta_logit, heads, first) for first in firsts]
    for first, (packed, *aux) in zip(firsts, locals_):
        near = neighbours(packed, odd)
        state = own_block(queries, keys, directions, values, aux, heads, first, size)
        state = remote_blocks(
            where, state, near[:2], near_values[:2], packed, (1, 2), False, heads, first, size
        )
        (attended,) = remote_blocks(
            where, state, near[2:], near_values[2:], near[1], (3, 4), True, heads, first, size
        )
        spread = [(0, attended)]
        bit = groups // 2
        while bit:
            spread += [(p ^ bit, swap(x, "head", bit)) for p, x in spread]
            bit //= 2
        for p, x in spread:
            gathered.append((x, first // heads))
            matching.append(weights[p])
    return project(gathered, matching)


def solution(mesh):
    return jax.shard_map(
        per_device,
        mesh=mesh,
        in_specs=(
            P("seq", "head"),
            P("seq", "head"),
            P("seq", "head"),
            P("seq", "head"),
            P("head", "seq"),
            P("head", None),
        ),
        out_specs=P("seq", "head"),
        check_vma=False,
    )
```

```python
import functools
import math

import jax
import jax.numpy as jnp
from jax import lax
from jax.experimental import pallas as pl
from jax.experimental.pallas import tpu as pltpu
from jax.sharding import PartitionSpec as P


SUB = 128
HEADS_AT_ONCE = 2
F32 = jnp.float32
BF16 = jnp.bfloat16
LOG2E = 1.0 / math.log(2.0)
MIB = 1 << 20


def split(x):
    high = x.astype(BF16)
    return high, (x - high.astype(F32)).astype(BF16)


def mm(a, b):
    return lax.dot_general(a, b, (((1,), (0,)), ((), ())), preferred_element_type=F32)


def mm_nt(a, b):
    return lax.dot_general(a, b, (((1,), (1,)), ((), ())), preferred_element_type=F32)


def mm_tn(a, b):
    return lax.dot_general(a, b, (((0,), (0,)), ((), ())), preferred_element_type=F32)


def dot3(a, b):
    (ah, al), (bh, bl) = split(a), split(b)
    return mm(jnp.concatenate([ah, al, ah], 1), jnp.concatenate([bh, bh, bl], 0))


def dot3_nt(a, b):
    (ah, al), (bh, bl) = split(a), split(b)
    return mm_nt(jnp.concatenate([ah, al, ah], 1), jnp.concatenate([bh, bh, bl], 1))


def dot2(a, b):
    ah, al = split(a)
    return mm(jnp.concatenate([ah, al], 1), jnp.concatenate([b, b], 0))


def iotas(size):
    rows = lax.broadcasted_iota(jnp.int32, (size, size), 0)
    cols = lax.broadcasted_iota(jnp.int32, (size, size), 1)
    return rows, cols


TINY = 16


def small_inverse(lower, rows, cols):
    count = SUB // TINY
    lanes = lax.broadcasted_iota(jnp.int32, (TINY, SUB), 1)
    inner = lax.broadcasted_iota(jnp.int32, (TINY, SUB), 0)
    packed = jnp.zeros((TINY, SUB), F32)
    for b in range(count):
        packed = jnp.where(lanes // TINY == b, lower[b * TINY : (b + 1) * TINY], packed)
    x = (lanes % TINY == inner).astype(F32)
    for j in range(TINY - 1):
        spread = jnp.take_along_axis(packed, lanes // TINY * TINY + j, axis=1)
        x = x - spread * x[j : j + 1]
    return jnp.where(rows // TINY == cols // TINY, jnp.concatenate([x] * count, 0), 0.0)


def local_kernel(heads, first, runs, direct, k_in, w_in, logit_in, kp_ref, coef_ref, mixed_ref, end_ref, map_ref, low, inv, gamma, hop, *own):
    k_ref, w_ref, logit_ref = k_in, w_in, logit_in
    arrivals = []
    if direct:
        k_ref, w_ref, logit_ref, sems = own
        lanes = pl.ds(first * (k_ref.shape[1] // heads), k_ref.shape[1])
        moves = ((logit_in, logit_ref), (w_in.at[:, lanes], w_ref), (k_in.at[:, lanes], k_ref))
        arrivals = [pltpu.make_async_copy(a, b, sems.at[i]) for i, (a, b) in enumerate(moves)]
        for copy in arrivals:
            copy.start()
        arrivals[0].wait()
        arrivals[1].wait()
    size = k_ref.shape[1] // heads
    length = runs * SUB
    rows, cols = iotas(SUB)
    eye = (rows == cols).astype(F32)
    units = [(h, r) for h in range(heads) for r in range(runs)]

    def at(ref, h, r):
        return ref[r * SUB : (r + 1) * SUB, h * size : (h + 1) * size]

    for u, (h, r) in enumerate(units):
        w = at(w_ref, h, r)
        gram = mm_nt(w, w)
        norm = jnp.sum(gram * eye, axis=0, keepdims=True)
        logit = logit_ref[first + h : first + h + 1, r * SUB : (r + 1) * SUB]
        strength = 2.0 * jax.nn.sigmoid(logit) / (norm + 1e-06)
        gamma[u] = jnp.broadcast_to(strength, (8, SUB))
        lower = jnp.where(rows > cols, gram * strength, 0.0)
        low[u] = lower
        inv[u] = small_inverse(lower, rows, cols)
    block = TINY
    while block < SUB:
        halves = range(block, SUB, 2 * block)
        mask = (cols // (2 * block) == rows // (2 * block)) & (rows // block != cols // block)
        picked = jnp.concatenate([mask[a : a + block] for a in halves], 0)
        for u in range(len(units)):
            x = inv[u]
            below = jnp.concatenate([x[a : a + block] for a in halves], 0)
            hop[u] = dot3(below, jnp.where(mask, low[u], 0.0))
        for u in range(len(units)):
            x = inv[u]
            below = jnp.concatenate([x[a : a + block] for a in halves], 0)
            step = dot3(hop[u], x)
            for i, a in enumerate(halves):
                inv[u, a : a + block, :] = below[i * block : (i + 1) * block] - step[i * block : (i + 1) * block]
        block *= 2
    for copy in arrivals[2:]:
        copy.wait()

    def put(ref, h, r, value):
        ref[r * SUB : (r + 1) * SUB, h * size : (h + 1) * size] = value

    for u, (h, r) in enumerate(units):
        strength = gamma[u][0:1]
        column = jnp.sum(eye * strength, axis=1, keepdims=True)
        put(coef_ref, h, r, dot2(inv[u], at(w_ref, h, r)) * column)
        low[u] = jnp.where(cols > rows, mm_nt(at(k_ref, h, r), at(w_ref, h, r)), 0.0)
    for u, (h, r) in enumerate(units):
        put(mixed_ref, h, r, dot3_nt(low[u], inv[u]) * gamma[u][0:1])
        w = at(w_ref, h, r)
        ch, cl = split(at(coef_ref, h, r))
        put(map_ref, h, r, eye - mm_tn(jnp.concatenate([w, w], 0), jnp.concatenate([ch, cl], 0)))
    for h, r in units:
        put(end_ref, h, r, at(k_ref, h, r).astype(F32) - dot2(at(mixed_ref, h, r), at(w_ref, h, r)))
    afters = [None] * heads
    for r in reversed(range(runs)):
        for h in range(heads):
            ends = at(end_ref, h, r)
            moved = ends if afters[h] is None else dot3_nt(ends, afters[h])
            put(kp_ref, h, r, moved.astype(BF16))
        for h in range(heads):
            run_map = at(map_ref, h, r)
            afters[h] = run_map if afters[h] is None else dot3(afters[h], run_map)
    for h in range(heads):
        kp_ref[length : length + size, h * size : (h + 1) * size] = afters[h].astype(BF16)


def local_keys(keys, directions, logits, heads, first, direct):
    length, width = keys.shape
    size = width // logits.shape[0]
    runs = length // SUB
    chunk = first // heads
    part = pl.BlockSpec((length, heads * size), lambda i: (0, chunk))
    whole = jax.ShapeDtypeStruct((length, heads * size), F32)
    units = heads * runs
    in_specs = [part, part, pl.BlockSpec(logits.shape, lambda i: (0, 0))]
    own = []
    if direct:
        in_specs = [pl.BlockSpec(memory_space=pltpu.HBM)] * 3
        keys, directions, logits = (pltpu.with_memory_space_constraint(x, pltpu.HBM) for x in (keys, directions, logits))
        own = [pltpu.VMEM((length, heads * size), BF16)] * 2
        own += [pltpu.VMEM(logits.shape, F32), pltpu.SemaphoreType.DMA((3,))]
    return pl.pallas_call(
        functools.partial(local_kernel, heads, first, runs, direct),
        grid=(1,),
        in_specs=in_specs,
        out_specs=[pl.BlockSpec((length + size, heads * size), lambda i: (0, 0))]
        + [pl.BlockSpec((length, heads * size), lambda i: (0, 0))] * 4,
        out_shape=[jax.ShapeDtypeStruct((length + size, heads * size), BF16), whole, whole, whole, whole],
        scratch_shapes=[
            pltpu.VMEM((units, SUB, SUB), F32),
            pltpu.VMEM((units, SUB, SUB), F32),
            pltpu.VMEM((units, 8, SUB), F32),
            pltpu.VMEM((units, SUB // 2, SUB), F32),
        ]
        + own,
        compiler_params=pltpu.CompilerParams(vmem_limit_bytes=24 * MIB),
        cost_estimate=pl.CostEstimate(
            flops=units * 60 * 2 * SUB**3 * 8, bytes_accessed=units * SUB * SUB * 24, transcendentals=0
        ),
        name="local_keys",
    )(keys, directions, logits)


def pack_stats(maxima, totals):
    lanes = lax.broadcasted_iota(jnp.int32, (maxima[0].shape[0], 128), 1)
    out = jnp.zeros(lanes.shape, F32)
    for i, column in enumerate(list(maxima) + list(totals)):
        out = jnp.where(lanes == i, column, out)
    return out


def own_kernel(heads, runs, q_ref, k_ref, w_ref, v_ref, coef_ref, mixed_ref, end_ref, map_ref, qt_ref, acc_ref, stat_ref, dirs, score, top_ref, sum_ref):
    size = q_ref.shape[1] // heads
    rows, cols = iotas(SUB)
    scale = LOG2E / math.sqrt(size)
    units = [(h, r) for r in range(runs) for h in range(heads)]

    def at(ref, h, r):
        return ref[r * SUB : (r + 1) * SUB, h * size : (h + 1) * size]

    def put(ref, h, r, value):
        ref[r * SUB : (r + 1) * SUB, h * size : (h + 1) * size] = value

    def keys(r):
        return slice(r * SUB, (r + 1) * SUB)

    for u, (h, r) in enumerate(units):
        found = mm_nt(at(q_ref, h, r), jnp.concatenate([at(w_ref, h, r), at(k_ref, h, r)], 0))
        dirs[u] = jnp.where(cols <= rows, found[:, :SUB], 0.0)
        score[u, :, keys(r)] = found[:, SUB:]
    for u, (h, r) in enumerate(units):
        put(qt_ref, h, r, at(q_ref, h, r).astype(F32) - dot3(dirs[u], at(coef_ref, h, r)))
        inside = score[u, :, keys(r)] - dot3_nt(dirs[u], at(mixed_ref, h, r))
        score[u, :, keys(r)] = jnp.where(cols <= rows, inside * scale, -jnp.inf)
    for back in range(1, runs):
        for u, (h, r) in enumerate(units):
            if r >= back:
                start = at(qt_ref, h, r)
                score[u, :, keys(r - back)] = dot3_nt(start, at(end_ref, h, r - back)) * scale
                put(qt_ref, h, r, dot3(start, at(map_ref, h, r - back)))
    for u, (h, r) in enumerate(units):
        put(qt_ref, h, r, at(qt_ref, h, r) * scale)
        top_ref[u] = jnp.broadcast_to(jnp.max(score[u, :, : (r + 1) * SUB], axis=1, keepdims=True), (SUB, SUB))
    for u, (h, r) in enumerate(units):
        weights = jnp.exp2(score[u, :, : (r + 1) * SUB] - top_ref[u][:, :1])
        sum_ref[u] = jnp.broadcast_to(jnp.sum(weights, axis=1, keepdims=True), (SUB, SUB))
        put(acc_ref, h, r, mm(weights.astype(BF16), v_ref[: (r + 1) * SUB, h * size : (h + 1) * size]))
    for r in range(runs):
        picked = [u for u, (_, other) in enumerate(units) if other == r]
        stat_ref[keys(r), :] = pack_stats([top_ref[u] for u in picked], [sum_ref[u] for u in picked])


def own_block(queries, keys, directions, values, aux, heads, first, size):
    length = queries.shape[0]
    runs = length // SUB
    chunk = first // heads
    part = pl.BlockSpec((length, heads * size), lambda i: (0, chunk))
    whole = pl.BlockSpec((length, heads * size), lambda i: (0, 0))
    units = heads * runs
    return pl.pallas_call(
        functools.partial(own_kernel, heads, runs),
        grid=(1,),
        in_specs=[part] * 4 + [whole] * 4,
        out_specs=[whole, whole, pl.BlockSpec((length, 128), lambda i: (0, 0))],
        out_shape=[jax.ShapeDtypeStruct((length, heads * size), F32)] * 2 + [jax.ShapeDtypeStruct((length, 128), F32)],
        scratch_shapes=[
            pltpu.VMEM((units, SUB, SUB), F32),
            pltpu.VMEM((units, SUB, length), F32),
            pltpu.VMEM((units, SUB, SUB), F32),
            pltpu.VMEM((units, SUB, SUB), F32),
        ],
        compiler_params=pltpu.CompilerParams(vmem_limit_bytes=24 * MIB),
        cost_estimate=pl.CostEstimate(
            flops=units * 25 * 2 * SUB**3 * 8, bytes_accessed=units * SUB * SUB * 32, transcendentals=0
        ),
        name="own_block",
    )(queries, keys, directions, values, *aux)


def remote_kernel(heads, runs, distances, last, position_ref, q_ref, acc_in, stat_in, *refs):
    total_count = len(distances)
    blocks, vals = refs[:total_count], refs[total_count : 2 * total_count]
    previous = refs[2 * total_count]
    outs = refs[2 * total_count + 1 :]
    size = q_ref.shape[1] // heads
    length = runs * SUB
    position = position_ref[0]

    def attend(count):
        stat = stat_in[...]
        maxima, totals = [], []
        for h in range(heads):
            span = slice(h * size, (h + 1) * size)
            q = q_ref[:, span]
            parts = []
            for i, distance in enumerate(distances[:count]):
                if distance > 1:
                    source = previous if i == 0 else blocks[i - 1]
                    q = dot2(q, source[length : length + size, span])
                qh, ql = split(q)
                kt = blocks[i][:length, span]
                parts.append(mm_nt(jnp.concatenate([qh, ql], 1), jnp.concatenate([kt, kt], 1)))
            old, total, acc = stat[:, h : h + 1], stat[:, heads + h : heads + h + 1], acc_in[:, span]
            top = old
            for part in parts:
                top = jnp.maximum(top, jnp.max(part, axis=1, keepdims=True))
            fade = jnp.exp2(old - top)
            total, acc = total * fade, acc * fade
            for i, part in enumerate(parts):
                weights = jnp.exp2(part - top)
                total += jnp.sum(weights, axis=1, keepdims=True)
                acc += mm(weights.astype(BF16), vals[i][:, span])
            if last:
                outs[0][:, span] = (acc / total).astype(BF16)
            else:
                outs[0][:, span] = q
                outs[1][:, span] = acc
                maxima.append(top)
                totals.append(total)
        if not last:
            outs[2][...] = pack_stats(maxima, totals)

    for count in range(total_count + 1):
        fits = True
        if count > 0:
            fits = position >= distances[count - 1]
        if count < total_count:
            fits = jnp.logical_and(fits, position < distances[count])
        pl.when(fits)(functools.partial(attend, count))


def remote_blocks(position, state, blocks, values, previous, distances, last, heads, first, size):
    q, acc, stat = state
    length = q.shape[0]
    runs = length // SUB
    chunk = first // heads
    whole = pl.BlockSpec((length, heads * size), lambda i: (0, 0))
    stats = pl.BlockSpec((length, 128), lambda i: (0, 0))
    part = pl.BlockSpec((length, heads * size), lambda i: (0, chunk))
    state_shape = jax.ShapeDtypeStruct((length, heads * size), F32)
    count = len(distances)
    if last:
        out_specs, out_shape = [whole], [jax.ShapeDtypeStruct((length, heads * size), BF16)]
    else:
        out_specs = [whole, whole, stats]
        out_shape = [state_shape, state_shape, jax.ShapeDtypeStruct((length, 128), F32)]
    return pl.pallas_call(
        functools.partial(remote_kernel, heads, runs, distances, last),
        grid=(1,),
        in_specs=[pl.BlockSpec(memory_space=pltpu.SMEM), whole, whole, stats]
        + [pl.BlockSpec(b.shape, lambda i: (0, 0)) for b in blocks]
        + [part] * count
        + [pl.BlockSpec(previous.shape, lambda i: (0, 0))],
        out_specs=out_specs,
        out_shape=out_shape,
        compiler_params=pltpu.CompilerParams(vmem_limit_bytes=24 * MIB),
        cost_estimate=pl.CostEstimate(
            flops=heads * runs * 60 * 2 * SUB**3, bytes_accessed=length * size * heads * 24, transcendentals=0
        ),
        name="remote_blocks",
    )(position, q, acc, stat, *blocks, *values, previous)


def project_kernel(count, base, *refs):
    rows, weights = refs[:count], refs[count : 2 * count]
    out = refs[-1]
    total = mm(rows[0][...], weights[0][...])
    for i in range(1, count):
        total += mm(rows[i][...], weights[i][...])
    if base:
        total += refs[2 * count][...]
    out[...] = total.astype(out.dtype)


def project(rows, weights, at, base, dtype):
    length, depth = rows[0].shape
    width = weights[0].shape[1]
    whole = pl.BlockSpec((length, width), lambda i: (0, 0))
    extra = [] if base is None else [base]
    return pl.pallas_call(
        functools.partial(project_kernel, len(rows), base is not None),
        grid=(1,),
        in_specs=[pl.BlockSpec(r.shape, lambda i: (0, 0)) for r in rows]
        + [pl.BlockSpec((depth, width), lambda i: (at, 0))] * len(rows)
        + [whole] * len(extra),
        out_specs=whole,
        out_shape=jax.ShapeDtypeStruct((length, width), dtype),
        compiler_params=pltpu.CompilerParams(vmem_limit_bytes=24 * MIB),
        cost_estimate=pl.CostEstimate(
            flops=2 * len(rows) * length * depth * width, bytes_accessed=4 * length * width, transcendentals=0
        ),
        name="project",
    )(*rows, *weights, *extra)


def ring(x, axis, distance):
    n = lax.axis_size(axis)
    return lax.ppermute(x, axis, [(i, (i + distance) % n) for i in range(n)])


def swap(x, axis, bit):
    n = lax.axis_size(axis)
    return lax.ppermute(x, axis, [(i, i ^ bit) for i in range(n)])


def neighbours(block, odd, relay_one, needed):
    two = ring(block, "seq", 2)
    one = swap(jnp.where(odd, two, block), "seq", 1)
    if relay_one:
        four = ring(two[:needed], "seq", 2)
        three = ring(one, "seq", 2)
        return one, two, three, four
    four = ring(two, "seq", 2)
    again = lax.optimization_barrier(two)
    three = swap(jnp.where(odd, four, again), "seq", 1)
    return one, two, three, four


def layer(queries, keys, values, directions, beta_logit, out_weight):
    length, width = queries.shape
    head_count = beta_logit.shape[0]
    size = width // head_count
    groups = lax.axis_size("head")
    heads = HEADS_AT_ONCE
    position = lax.axis_index("seq")
    group = lax.axis_index("head")
    odd = position % 2 == 1
    where = jnp.reshape(position, (1,)).astype(jnp.int32)

    near_values = neighbours(values, odd, False, length)
    columns = out_weight.shape[1] // groups
    weights = []
    for p in range(groups):
        piece = lax.dynamic_slice_in_dim(out_weight, (group ^ p) * columns, columns, 1)
        weights.append(piece if p == 0 else swap(piece, "head", p))

    mixed = None
    for c, first in enumerate(range(0, head_count, heads)):
        packed, *aux = local_keys(keys, directions, beta_logit, heads, first, c == 0)
        near = neighbours(packed, odd, c > 0, length)
        state = own_block(queries, keys, directions, values, aux, heads, first, size)
        state = remote_blocks(
            where, state, near[:2], near_values[:2], packed, (1, 2), False, heads, first, size
        )
        (attended,) = remote_blocks(where, state, near[2:], near_values[2:], near[1], (3, 4), True, heads, first, size)
        spread = [(0, attended)]
        bit = groups // 2
        while bit:
            spread += [(p ^ bit, swap(x, "head", bit)) for p, x in spread]
            bit //= 2
        done = first + heads == head_count
        rows, blocks = [x for _, x in spread], [weights[p] for p, _ in spread]
        mixed = project(rows, blocks, c, mixed, BF16 if done else F32)
    return mixed


def solution(mesh):
    return jax.shard_map(
        layer,
        mesh=mesh,
        in_specs=(
            P("seq", "head"),
            P("seq", "head"),
            P("seq", "head"),
            P("seq", "head"),
            P("head", "seq"),
            P("head", None),
        ),
        out_specs=P("seq", "head"),
        check_vma=False,
    )
```

```python
import functools
import math

import jax
import jax.numpy as jnp
from jax import lax
from jax.experimental import pallas as pl
from jax.experimental.pallas import tpu as pltpu
from jax.sharding import PartitionSpec as P


SUB = 128
HEADS_AT_ONCE = 2
F32 = jnp.float32
BF16 = jnp.bfloat16
LOG2E = 1.0 / math.log(2.0)
MIB = 1 << 20


def split(x):
    high = x.astype(BF16)
    return high, (x - high.astype(F32)).astype(BF16)


def mm(a, b):
    return lax.dot_general(a, b, (((1,), (0,)), ((), ())), preferred_element_type=F32)


def mm_nt(a, b):
    return lax.dot_general(a, b, (((1,), (1,)), ((), ())), preferred_element_type=F32)


def mm_tn(a, b):
    return lax.dot_general(a, b, (((0,), (0,)), ((), ())), preferred_element_type=F32)


def dot3(a, b):
    (ah, al), (bh, bl) = split(a), split(b)
    return mm(jnp.concatenate([ah, al, ah], 1), jnp.concatenate([bh, bh, bl], 0))


def dot3_nt(a, b):
    (ah, al), (bh, bl) = split(a), split(b)
    return mm_nt(jnp.concatenate([ah, al, ah], 1), jnp.concatenate([bh, bh, bl], 1))


def dot2(a, b):
    ah, al = split(a)
    return mm(jnp.concatenate([ah, al], 1), jnp.concatenate([b, b], 0))


def iotas(size):
    rows = lax.broadcasted_iota(jnp.int32, (size, size), 0)
    cols = lax.broadcasted_iota(jnp.int32, (size, size), 1)
    return rows, cols


TINY = 16


def small_inverse(lower, rows, cols):
    count = SUB // TINY
    lanes = lax.broadcasted_iota(jnp.int32, (TINY, SUB), 1)
    inner = lax.broadcasted_iota(jnp.int32, (TINY, SUB), 0)
    packed = jnp.zeros((TINY, SUB), F32)
    for b in range(count):
        packed = jnp.where(lanes // TINY == b, lower[b * TINY : (b + 1) * TINY], packed)
    x = (lanes % TINY == inner).astype(F32)
    for j in range(TINY - 1):
        spread = jnp.take_along_axis(packed, lanes // TINY * TINY + j, axis=1)
        x = x - spread * x[j : j + 1]
    return jnp.where(rows // TINY == cols // TINY, jnp.concatenate([x] * count, 0), 0.0)


def pack_stats(maxima, totals):
    lanes = lax.broadcasted_iota(jnp.int32, (maxima[0].shape[0], 128), 1)
    out = jnp.zeros(lanes.shape, F32)
    for i, column in enumerate(list(maxima) + list(totals)):
        out = jnp.where(lanes == i, column, out)
    return out


def local_kernel(heads, chunks, *refs):
    count = 4 * chunks
    inputs, results, (low, inv, gamma, hop, score, tops, sums), (coef, mixed, ends, maps), buffers, sems = (
        refs[:5], refs[5 : 5 + count], refs[5 + count : 12 + count], refs[12 + count : 16 + count], refs[16 + count : -1], refs[-1]
    )
    packed, moved_queries, accs, stats = (results[i::4] for i in range(4))
    arrivals = [pltpu.make_async_copy(a, b, sems.at[i]) for i, (a, b) in enumerate(zip(inputs, buffers))]
    for copy in arrivals:
        copy.start()
    logit_ref, w_ref, k_ref, q_ref, v_ref = buffers
    length, width = k_ref.shape
    size = width // (heads * chunks)
    runs = length // SUB
    rows, cols = iotas(SUB)
    eye = (rows == cols).astype(F32)
    scale = LOG2E / math.sqrt(size)
    units = [(h, r) for h in range(heads * chunks) for r in range(runs)]

    def at(ref, h, r):
        if isinstance(ref, tuple):
            ref, h = ref[h // heads], h % heads
        return ref[r * SUB : (r + 1) * SUB, h * size : (h + 1) * size]

    def put(ref, h, r, value):
        if isinstance(ref, tuple):
            ref, h = ref[h // heads], h % heads
        ref[r * SUB : (r + 1) * SUB, h * size : (h + 1) * size] = value

    def keys(r):
        return slice(r * SUB, (r + 1) * SUB)

    arrivals[0].wait()
    arrivals[1].wait()
    for u, (h, r) in enumerate(units):
        w = at(w_ref, h, r)
        gram = mm_nt(w, w)
        norm = jnp.sum(gram * eye, axis=0, keepdims=True)
        logit = logit_ref[h : h + 1, r * SUB : (r + 1) * SUB]
        strength = 2.0 * jax.nn.sigmoid(logit) / (norm + 1e-06)
        gamma[u] = jnp.broadcast_to(strength, (8, SUB))
        low[u] = jnp.where(rows > cols, gram * strength, 0.0)
    for u in range(len(units)):
        inv[u] = small_inverse(low[u], rows, cols)
    block = TINY
    while block < SUB:
        halves = range(block, SUB, 2 * block)
        mask = (cols // (2 * block) == rows // (2 * block)) & (rows // block != cols // block)
        for u in range(len(units)):
            x = inv[u]
            below = jnp.concatenate([x[a : a + block] for a in halves], 0)
            hop[u] = dot3(below, jnp.where(mask, low[u], 0.0))
        for u in range(len(units)):
            x = inv[u]
            below = jnp.concatenate([x[a : a + block] for a in halves], 0)
            step = dot3(hop[u], x)
            for i, a in enumerate(halves):
                inv[u, a : a + block, :] = below[i * block : (i + 1) * block] - step[i * block : (i + 1) * block]
        block *= 2
    arrivals[2].wait()
    for u, (h, r) in enumerate(units):
        column = jnp.sum(eye * gamma[u][0:1], axis=1, keepdims=True)
        put(coef, h, r, dot2(inv[u], at(w_ref, h, r)) * column)
        low[u] = jnp.where(cols > rows, mm_nt(at(k_ref, h, r), at(w_ref, h, r)), 0.0)
    for u, (h, r) in enumerate(units):
        put(mixed, h, r, dot3_nt(low[u], inv[u]) * gamma[u][0:1])
        w = at(w_ref, h, r)
        ch, cl = split(at(coef, h, r))
        put(maps, h, r, eye - mm_tn(jnp.concatenate([w, w], 0), jnp.concatenate([ch, cl], 0)))
    for h, r in units:
        put(ends, h, r, at(k_ref, h, r).astype(F32) - dot2(at(mixed, h, r), at(w_ref, h, r)))
    afters = [None] * (heads * chunks)
    for r in reversed(range(runs)):
        for h in range(heads * chunks):
            moved = at(ends, h, r)
            if afters[h] is not None:
                moved = dot3_nt(moved, afters[h])
            put(packed, h, r, moved.astype(BF16))
        for h in range(heads * chunks):
            run_map = at(maps, h, r)
            afters[h] = run_map if afters[h] is None else dot3(afters[h], run_map)
    for h in range(heads * chunks):
        span = slice(h % heads * size, (h % heads + 1) * size)
        packed[h // heads][length : length + size, span] = afters[h].astype(BF16)

    arrivals[3].wait()
    for u, (h, r) in enumerate(units):
        found = mm_nt(at(q_ref, h, r), jnp.concatenate([at(w_ref, h, r), at(k_ref, h, r)], 0))
        low[u] = jnp.where(cols <= rows, found[:, :SUB], 0.0)
        score[u, :, keys(r)] = found[:, SUB:]
    for u, (h, r) in enumerate(units):
        put(moved_queries, h, r, at(q_ref, h, r).astype(F32) - dot3(low[u], at(coef, h, r)))
        inside = score[u, :, keys(r)] - dot3_nt(low[u], at(mixed, h, r))
        score[u, :, keys(r)] = jnp.where(cols <= rows, inside * scale, -jnp.inf)
    for back in range(1, runs):
        for u, (h, r) in enumerate(units):
            if r >= back:
                start = at(moved_queries, h, r)
                score[u, :, keys(r - back)] = dot3_nt(start, at(ends, h, r - back)) * scale
                put(moved_queries, h, r, dot3(start, at(maps, h, r - back)))
    for u, (h, r) in enumerate(units):
        put(moved_queries, h, r, at(moved_queries, h, r) * scale)
        tops[u] = jnp.broadcast_to(jnp.max(score[u, :, : (r + 1) * SUB], axis=1, keepdims=True), (SUB, SUB))
    arrivals[4].wait()
    for u, (h, r) in enumerate(units):
        weights = jnp.exp2(score[u, :, : (r + 1) * SUB] - tops[u][:, :1])
        sums[u] = jnp.broadcast_to(jnp.sum(weights, axis=1, keepdims=True), (SUB, SUB))
        put(accs, h, r, mm(weights.astype(BF16), v_ref[: (r + 1) * SUB, h * size : (h + 1) * size]))
    for c in range(chunks):
        for r in range(runs):
            picked = [u for u, (h, other) in enumerate(units) if other == r and h // heads == c]
            stats[c][keys(r), :] = pack_stats([tops[u] for u in picked], [sums[u] for u in picked])


def local_pass(queries, keys, values, directions, logits, heads):
    length, width = keys.shape
    head_count = logits.shape[0]
    chunks = head_count // heads
    size = width // head_count
    units = head_count * (length // SUB)
    shapes = [jax.ShapeDtypeStruct((length + size, heads * size), BF16)]
    shapes += [jax.ShapeDtypeStruct((length, heads * size), F32)] * 2
    shapes += [jax.ShapeDtypeStruct((length, 128), F32)]
    operands = [pltpu.with_memory_space_constraint(x, pltpu.HBM) for x in (logits, directions, keys, queries, values)]
    tile = pltpu.VMEM((units, SUB, SUB), F32)
    out = pl.pallas_call(
        functools.partial(local_kernel, heads, chunks),
        grid=(1,),
        in_specs=[pl.BlockSpec(memory_space=pltpu.HBM)] * 5,
        out_specs=[pl.BlockSpec(x.shape, lambda i: (0, 0)) for x in shapes] * chunks,
        out_shape=shapes * chunks,
        scratch_shapes=[
            tile,
            tile,
            pltpu.VMEM((units, 8, SUB), F32),
            pltpu.VMEM((units, SUB // 2, SUB), F32),
            pltpu.VMEM((units, SUB, length), F32),
            tile,
            tile,
        ]
        + [pltpu.VMEM((length, width), F32)] * 4
        + [pltpu.VMEM(logits.shape, F32)]
        + [pltpu.VMEM((length, width), BF16)] * 4
        + [pltpu.SemaphoreType.DMA((5,))],
        compiler_params=pltpu.CompilerParams(vmem_limit_bytes=28 * MIB),
        cost_estimate=pl.CostEstimate(
            flops=units * 90 * 2 * SUB**3 * 8, bytes_accessed=units * SUB * SUB * 24, transcendentals=0
        ),
        name="local_pass",
    )(*operands)
    return [out[4 * c : 4 * c + 4] for c in range(chunks)]


def attend(heads, count, query, blocks, vals, acc_in, stat_in, acc_out, stat_out):
    length, width = acc_in.shape
    size = width // heads
    stat = stat_in[...]
    tops, sums = [], []
    for h in range(heads):
        span = slice(h * size, (h + 1) * size)
        parts = []
        for i in range(count):
            qh, ql = split(query(i, span))
            kt = blocks[i][:length, span]
            parts.append(mm_nt(jnp.concatenate([qh, ql], 1), jnp.concatenate([kt, kt], 1)))
        old, total, acc = stat[:, h : h + 1], stat[:, heads + h : heads + h + 1], acc_in[:, span]
        top = old
        for part in parts:
            top = jnp.maximum(top, jnp.max(part, axis=1, keepdims=True))
        if count:
            fade = jnp.exp2(old - top)
            total, acc = total * fade, acc * fade
        for i, part in enumerate(parts):
            weights = jnp.exp2(part - top)
            total += jnp.sum(weights, axis=1, keepdims=True)
            acc += mm(weights.astype(BF16), vals[i][:, span])
        if stat_out is None:
            acc_out[:, span] = (acc / total).astype(BF16)
        else:
            acc_out[:, span] = acc
            tops.append(top)
            sums.append(total)
    if stat_out is not None:
        stat_out[...] = pack_stats(tops, sums)


def within(position, distances, run):
    for count in range(len(distances) + 1):
        fits = position >= distances[count - 1] if count else True
        if count < len(distances):
            fits = jnp.logical_and(fits, position < distances[count])
        pl.when(fits)(functools.partial(run, count))


def near_kernel(heads, mixes, position_ref, q_ref, acc_in, stat_in, one, two, v_one, v_two, acc_out, stat_out, *queries):
    length, width = q_ref.shape
    size = width // heads
    position = position_ref[0]
    second, third, relay = queries[0], queries[1], queries[-1]

    def run(count):
        for h in range(heads):
            span = slice(h * size, (h + 1) * size)
            block_map = one[length : length + size, span]
            relay[:, span] = mm_nt(two[:length, span], block_map).astype(BF16)
            second[:, span] = dot2(q_ref[:, span], block_map)
            third[:, span] = dot2(second[:, span], two[length : length + size, span])
            if mixes:
                queries[2][:, span] = jnp.where(position % 2 == 1, third[:, span], second[:, span])
        refs = (q_ref, second)
        attend(heads, count, lambda i, span: refs[i][:, span], (one, two), (v_one, v_two), acc_in, stat_in, acc_out, stat_out)

    within(position, (1, 2), run)


def far_kernel(heads, distance, last, position_ref, q_ref, acc_in, stat_in, block, vals, acc_out, *stat_out):
    def run(count):
        attend(heads, count, lambda i, span: q_ref[:, span], (block,), (vals,), acc_in, stat_in, acc_out, None if last else stat_out[0])

    within(position_ref[0], (distance,), run)


def whole(shape):
    return pl.BlockSpec(shape, lambda i: (0, 0))


def near_blocks(position, state, one, two, v_one, v_two, heads, chunk, mixes):
    length, width = state[0].shape
    part = pl.BlockSpec((length, width), lambda i: (0, chunk))
    shapes = [jax.ShapeDtypeStruct((length, width), F32), jax.ShapeDtypeStruct((length, 128), F32)]
    shapes += [jax.ShapeDtypeStruct((length, width), F32)] * (3 if mixes else 2)
    shapes += [jax.ShapeDtypeStruct((length, width), BF16)]
    return pl.pallas_call(
        functools.partial(near_kernel, heads, mixes),
        grid=(1,),
        in_specs=[pl.BlockSpec(memory_space=pltpu.SMEM)]
        + [whole(x.shape) for x in state]
        + [whole(one.shape), whole(two.shape), part, part],
        out_specs=[whole(x.shape) for x in shapes],
        out_shape=shapes,
        compiler_params=pltpu.CompilerParams(vmem_limit_bytes=24 * MIB),
        cost_estimate=pl.CostEstimate(
            flops=14 * length * length * width, bytes_accessed=length * width * 30, transcendentals=0
        ),
        name="near_blocks",
    )(position, *state, one, two, v_one, v_two)


def far_block(position, query, acc, stat, block, values, heads, chunk, distance, last):
    length, width = acc.shape
    shapes = [jax.ShapeDtypeStruct((length, width), BF16 if last else F32)]
    shapes += [] if last else [jax.ShapeDtypeStruct((length, 128), F32)]
    operands = (query, acc, stat, block)
    return pl.pallas_call(
        functools.partial(far_kernel, heads, distance, last),
        grid=(1,),
        in_specs=[pl.BlockSpec(memory_space=pltpu.SMEM)]
        + [whole(x.shape) for x in operands]
        + [pl.BlockSpec((length, width), lambda i: (0, chunk))],
        out_specs=[whole(x.shape) for x in shapes],
        out_shape=shapes,
        compiler_params=pltpu.CompilerParams(vmem_limit_bytes=24 * MIB),
        cost_estimate=pl.CostEstimate(
            flops=6 * length * length * width, bytes_accessed=length * width * 20, transcendentals=0
        ),
        name="far_block",
    )(position, *operands, values)


def project_kernel(count, base, *refs):
    rows, weights = refs[:count], refs[count : 2 * count]
    out = refs[-1]
    total = mm(rows[0][...], weights[0][...])
    for i in range(1, count):
        total += mm(rows[i][...], weights[i][...])
    if base:
        total += refs[2 * count][...]
    out[...] = total.astype(out.dtype)


def project(rows, weights, at, base, dtype):
    length, depth = rows[0].shape
    width = weights[0].shape[1]
    whole = pl.BlockSpec((length, width), lambda i: (0, 0))
    extra = [] if base is None else [base]
    return pl.pallas_call(
        functools.partial(project_kernel, len(rows), base is not None),
        grid=(1,),
        in_specs=[pl.BlockSpec(r.shape, lambda i: (0, 0)) for r in rows]
        + [pl.BlockSpec((depth, width), lambda i: (at, 0))] * len(rows)
        + [whole] * len(extra),
        out_specs=whole,
        out_shape=jax.ShapeDtypeStruct((length, width), dtype),
        compiler_params=pltpu.CompilerParams(vmem_limit_bytes=14 * MIB),
        cost_estimate=pl.CostEstimate(
            flops=2 * len(rows) * length * depth * width, bytes_accessed=4 * length * width, transcendentals=0
        ),
        name="project",
    )(*rows, *weights, *extra)


def ring(x, axis, distance):
    n = lax.axis_size(axis)
    return lax.ppermute(x, axis, [(i, (i + distance) % n) for i in range(n)])


def swap(x, axis, bit):
    n = lax.axis_size(axis)
    return lax.ppermute(x, axis, [(i, i ^ bit) for i in range(n)])


def relayed(block, odd):
    two = ring(block, "seq", 2)
    one = swap(jnp.where(odd, two, block), "seq", 1)
    return one, two


def crossed(two, four, odd):
    again = lax.optimization_barrier(two)
    return swap(jnp.where(odd, four, again), "seq", 1)


def layer(queries, keys, values, directions, beta_logit, out_weight):
    length, _ = queries.shape
    groups = lax.axis_size("head")
    heads = HEADS_AT_ONCE
    position = lax.axis_index("seq")
    group = lax.axis_index("head")
    odd = position % 2 == 1
    where = jnp.reshape(position, (1,)).astype(jnp.int32)

    v_one, v_two = relayed(values, odd)
    v_four = ring(v_two, "seq", 2)
    v_three = crossed(v_two, v_four, odd)
    columns = out_weight.shape[1] // groups
    weights = []
    for p in range(groups):
        piece = lax.dynamic_slice_in_dim(out_weight, (group ^ p) * columns, columns, 1)
        weights.append(piece if p == 0 else swap(piece, "head", p))

    mixed = None
    locals_ = local_pass(queries, keys, values, directions, beta_logit, heads)
    for c, (packed, *state) in enumerate(locals_):
        one, two = relayed(packed, odd)
        mixes = c == 0
        acc, stat, _, *queries, relay = near_blocks(where, state, one, two, v_one, v_two, heads, c, mixes)
        four = ring(relay, "seq", 2)
        if mixes:
            three = crossed(two[:length], four, odd)
        else:
            three = ring(one[:length], "seq", 2)
        acc, stat = far_block(where, queries[0], acc, stat, four, v_four, heads, c, 4, False)
        (attended,) = far_block(where, queries[-1], acc, stat, three, v_three, heads, c, 3, True)
        spread = [(0, attended)]
        bit = groups // 2
        while bit:
            spread += [(p ^ bit, swap(x, "head", bit)) for p, x in spread]
            bit //= 2
        done = c + 1 == len(locals_)
        rows, blocks = [x for _, x in spread], [weights[p] for p, _ in spread]
        mixed = project(rows, blocks, c, mixed, BF16 if done else F32)
    return mixed


def solution(mesh):
    return jax.shard_map(
        layer,
        mesh=mesh,
        in_specs=(
            P("seq", "head"),
            P("seq", "head"),
            P("seq", "head"),
            P("seq", "head"),
            P("head", "seq"),
            P("head", None),
        ),
        out_specs=P("seq", "head"),
        check_vma=False,
    )
```

```python
import functools
import math

import jax
import jax.numpy as jnp
from jax import lax
from jax.experimental import pallas as pl
from jax.experimental.pallas import tpu as pltpu
from jax.sharding import PartitionSpec as P


SUB = 128
HEADS_AT_ONCE = 2
F32 = jnp.float32
BF16 = jnp.bfloat16
LOG2E = 1.0 / math.log(2.0)
MIB = 1 << 20


def split(x):
    high = x.astype(BF16)
    return high, (x - high.astype(F32)).astype(BF16)


def mm(a, b):
    return lax.dot_general(a, b, (((1,), (0,)), ((), ())), preferred_element_type=F32)


def mm_nt(a, b):
    return lax.dot_general(a, b, (((1,), (1,)), ((), ())), preferred_element_type=F32)


def mm_tn(a, b):
    return lax.dot_general(a, b, (((0,), (0,)), ((), ())), preferred_element_type=F32)


def dot3(a, b):
    (ah, al), (bh, bl) = split(a), split(b)
    return mm(jnp.concatenate([ah, al, ah], 1), jnp.concatenate([bh, bh, bl], 0))


def dot3_nt(a, b):
    (ah, al), (bh, bl) = split(a), split(b)
    return mm_nt(jnp.concatenate([ah, al, ah], 1), jnp.concatenate([bh, bh, bl], 1))


def dot2(a, b):
    ah, al = split(a)
    return mm(jnp.concatenate([ah, al], 1), jnp.concatenate([b, b], 0))


def iotas(size):
    rows = lax.broadcasted_iota(jnp.int32, (size, size), 0)
    cols = lax.broadcasted_iota(jnp.int32, (size, size), 1)
    return rows, cols


TINY = 16


def small_inverse(lower, rows, cols):
    count = SUB // TINY
    lanes = lax.broadcasted_iota(jnp.int32, (TINY, SUB), 1)
    inner = lax.broadcasted_iota(jnp.int32, (TINY, SUB), 0)
    packed = jnp.zeros((TINY, SUB), F32)
    for b in range(count):
        packed = jnp.where(lanes // TINY == b, lower[b * TINY : (b + 1) * TINY], packed)
    x = (lanes % TINY == inner).astype(F32)
    for j in range(TINY - 1):
        spread = jnp.take_along_axis(packed, lanes // TINY * TINY + j, axis=1)
        x = x - spread * x[j : j + 1]
    return jnp.where(rows // TINY == cols // TINY, jnp.concatenate([x] * count, 0), 0.0)


def pack_stats(maxima, totals):
    lanes = lax.broadcasted_iota(jnp.int32, (maxima[0].shape[0], 128), 1)
    out = jnp.zeros(lanes.shape, F32)
    for i, column in enumerate(list(maxima) + list(totals)):
        out = jnp.where(lanes == i, column, out)
    return out


def local_kernel(heads, chunks, *refs):
    count = 4 * chunks
    inputs, results, (low, inv, gamma, hop, score, tops, sums), (coef, mixed, ends, maps), buffers, sems = (
        refs[:5], refs[5 : 5 + count], refs[5 + count : 12 + count], refs[12 + count : 16 + count], refs[16 + count : -1], refs[-1]
    )
    packed, moved_queries, accs, stats = (results[i::4] for i in range(4))
    arrivals = [pltpu.make_async_copy(a, b, sems.at[i]) for i, (a, b) in enumerate(zip(inputs, buffers))]
    for copy in arrivals:
        copy.start()
    logit_ref, w_ref, k_ref, q_ref, v_ref = buffers
    length, width = k_ref.shape
    size = width // (heads * chunks)
    runs = length // SUB
    rows, cols = iotas(SUB)
    eye = (rows == cols).astype(F32)
    scale = LOG2E / math.sqrt(size)
    units = [(h, r) for h in range(heads * chunks) for r in range(runs)]

    def at(ref, h, r):
        if isinstance(ref, tuple):
            ref, h = ref[h // heads], h % heads
        return ref[r * SUB : (r + 1) * SUB, h * size : (h + 1) * size]

    def put(ref, h, r, value):
        if isinstance(ref, tuple):
            ref, h = ref[h // heads], h % heads
        ref[r * SUB : (r + 1) * SUB, h * size : (h + 1) * size] = value

    def keys(r):
        return slice(r * SUB, (r + 1) * SUB)

    arrivals[0].wait()
    arrivals[1].wait()
    for u, (h, r) in enumerate(units):
        w = at(w_ref, h, r)
        gram = mm_nt(w, w)
        norm = jnp.sum(gram * eye, axis=0, keepdims=True)
        logit = logit_ref[h : h + 1, r * SUB : (r + 1) * SUB]
        strength = 2.0 * jax.nn.sigmoid(logit) / (norm + 1e-06)
        gamma[u] = jnp.broadcast_to(strength, (8, SUB))
        low[u] = jnp.where(rows > cols, gram * strength, 0.0)
    for u in range(len(units)):
        inv[u] = small_inverse(low[u], rows, cols)
    block = TINY
    while block < SUB:
        halves = range(block, SUB, 2 * block)
        mask = (cols // (2 * block) == rows // (2 * block)) & (rows // block != cols // block)
        for u in range(len(units)):
            x = inv[u]
            below = jnp.concatenate([x[a : a + block] for a in halves], 0)
            hop[u] = dot3(below, jnp.where(mask, low[u], 0.0))
        for u in range(len(units)):
            x = inv[u]
            below = jnp.concatenate([x[a : a + block] for a in halves], 0)
            step = dot3(hop[u], x)
            for i, a in enumerate(halves):
                inv[u, a : a + block, :] = below[i * block : (i + 1) * block] - step[i * block : (i + 1) * block]
        block *= 2
    arrivals[2].wait()
    for u, (h, r) in enumerate(units):
        column = jnp.sum(eye * gamma[u][0:1], axis=1, keepdims=True)
        put(coef, h, r, dot2(inv[u], at(w_ref, h, r)) * column)
        low[u] = jnp.where(cols > rows, mm_nt(at(k_ref, h, r), at(w_ref, h, r)), 0.0)
    for u, (h, r) in enumerate(units):
        put(mixed, h, r, dot3_nt(low[u], inv[u]) * gamma[u][0:1])
        w = at(w_ref, h, r)
        ch, cl = split(at(coef, h, r))
        put(maps, h, r, eye - mm_tn(jnp.concatenate([w, w], 0), jnp.concatenate([ch, cl], 0)))
    for h, r in units:
        put(ends, h, r, at(k_ref, h, r).astype(F32) - dot2(at(mixed, h, r), at(w_ref, h, r)))
    afters = [None] * (heads * chunks)
    for r in reversed(range(runs)):
        for h in range(heads * chunks):
            moved = at(ends, h, r)
            if afters[h] is not None:
                moved = dot3_nt(moved, afters[h])
            put(packed, h, r, moved.astype(BF16))
        for h in range(heads * chunks):
            run_map = at(maps, h, r)
            afters[h] = run_map if afters[h] is None else dot3(afters[h], run_map)
    for h in range(heads * chunks):
        span = slice(h % heads * size, (h % heads + 1) * size)
        packed[h // heads][length : length + size, span] = afters[h].astype(BF16)

    arrivals[3].wait()
    for u, (h, r) in enumerate(units):
        found = mm_nt(at(q_ref, h, r), jnp.concatenate([at(w_ref, h, r), at(k_ref, h, r)], 0))
        low[u] = jnp.where(cols <= rows, found[:, :SUB], 0.0)
        score[u, :, keys(r)] = found[:, SUB:]
    for u, (h, r) in enumerate(units):
        put(moved_queries, h, r, at(q_ref, h, r).astype(F32) - dot3(low[u], at(coef, h, r)))
        inside = score[u, :, keys(r)] - dot3_nt(low[u], at(mixed, h, r))
        score[u, :, keys(r)] = jnp.where(cols <= rows, inside * scale, -jnp.inf)
    for back in range(1, runs):
        for u, (h, r) in enumerate(units):
            if r >= back:
                start = at(moved_queries, h, r)
                score[u, :, keys(r - back)] = dot3_nt(start, at(ends, h, r - back)) * scale
                put(moved_queries, h, r, dot3(start, at(maps, h, r - back)))
    for u, (h, r) in enumerate(units):
        put(moved_queries, h, r, at(moved_queries, h, r) * scale)
        tops[u] = jnp.broadcast_to(jnp.max(score[u, :, : (r + 1) * SUB], axis=1, keepdims=True), (SUB, SUB))
    arrivals[4].wait()
    for u, (h, r) in enumerate(units):
        weights = jnp.exp2(score[u, :, : (r + 1) * SUB] - tops[u][:, :1])
        sums[u] = jnp.broadcast_to(jnp.sum(weights, axis=1, keepdims=True), (SUB, SUB))
        put(accs, h, r, mm(weights.astype(BF16), v_ref[: (r + 1) * SUB, h * size : (h + 1) * size]))
    for c in range(chunks):
        for r in range(runs):
            picked = [u for u, (h, other) in enumerate(units) if other == r and h // heads == c]
            stats[c][keys(r), :] = pack_stats([tops[u] for u in picked], [sums[u] for u in picked])


def local_pass(queries, keys, values, directions, logits, heads):
    length, width = keys.shape
    head_count = logits.shape[0]
    chunks = head_count // heads
    size = width // head_count
    units = head_count * (length // SUB)
    shapes = [jax.ShapeDtypeStruct((length + size, heads * size), BF16)]
    shapes += [jax.ShapeDtypeStruct((length, heads * size), F32)] * 2
    shapes += [jax.ShapeDtypeStruct((length, 128), F32)]
    operands = [pltpu.with_memory_space_constraint(x, pltpu.HBM) for x in (logits, directions, keys, queries, values)]
    tile = pltpu.VMEM((units, SUB, SUB), F32)
    out = pl.pallas_call(
        functools.partial(local_kernel, heads, chunks),
        grid=(1,),
        in_specs=[pl.BlockSpec(memory_space=pltpu.HBM)] * 5,
        out_specs=[pl.BlockSpec(x.shape, lambda i: (0, 0)) for x in shapes] * chunks,
        out_shape=shapes * chunks,
        scratch_shapes=[
            tile,
            tile,
            pltpu.VMEM((units, 8, SUB), F32),
            pltpu.VMEM((units, SUB // 2, SUB), F32),
            pltpu.VMEM((units, SUB, length), F32),
            tile,
            tile,
        ]
        + [pltpu.VMEM((length, width), F32)] * 4
        + [pltpu.VMEM(logits.shape, F32)]
        + [pltpu.VMEM((length, width), BF16)] * 4
        + [pltpu.SemaphoreType.DMA((5,))],
        compiler_params=pltpu.CompilerParams(vmem_limit_bytes=28 * MIB),
        cost_estimate=pl.CostEstimate(
            flops=units * 90 * 2 * SUB**3 * 8, bytes_accessed=units * SUB * SUB * 24, transcendentals=0
        ),
        name="local_pass",
    )(*operands)
    return [out[4 * c : 4 * c + 4] for c in range(chunks)]


def attend(heads, count, query, blocks, vals, acc_in, stat_in, acc_out, stat_out):
    length, width = acc_in.shape
    size = width // heads
    stat = stat_in[...]
    tops, sums = [], []
    for h in range(heads):
        span = slice(h * size, (h + 1) * size)
        parts = []
        for i in range(count):
            qh, ql = split(query(i, span))
            kt = blocks[i][:length, span]
            parts.append(mm_nt(jnp.concatenate([qh, ql], 1), jnp.concatenate([kt, kt], 1)))
        old, total, acc = stat[:, h : h + 1], stat[:, heads + h : heads + h + 1], acc_in[:, span]
        top = old
        for part in parts:
            top = jnp.maximum(top, jnp.max(part, axis=1, keepdims=True))
        if count:
            fade = jnp.exp2(old - top)
            total, acc = total * fade, acc * fade
        for i, part in enumerate(parts):
            weights = jnp.exp2(part - top)
            total += jnp.sum(weights, axis=1, keepdims=True)
            acc += mm(weights.astype(BF16), vals[i][:, span])
        if stat_out is None:
            acc_out[:, span] = (acc / total).astype(BF16)
        else:
            acc_out[:, span] = acc
            tops.append(top)
            sums.append(total)
    if stat_out is not None:
        stat_out[...] = pack_stats(tops, sums)


def within(position, distances, run):
    for count in range(len(distances) + 1):
        fits = position >= distances[count - 1] if count else True
        if count < len(distances):
            fits = jnp.logical_and(fits, position < distances[count])
        pl.when(fits)(functools.partial(run, count))


def near_kernel(heads, mixes, position_ref, q_ref, acc_in, stat_in, one, two, v_one, v_two, acc_out, stat_out, *queries):
    length, width = q_ref.shape
    size = width // heads
    position = position_ref[0]
    second, third, relay = queries[0], queries[1], queries[-1]

    def run(count):
        for h in range(heads):
            span = slice(h * size, (h + 1) * size)
            block_map = one[length : length + size, span]
            relay[:, span] = mm_nt(two[:length, span], block_map).astype(BF16)
            second[:, span] = dot2(q_ref[:, span], block_map)
            third[:, span] = dot2(second[:, span], two[length : length + size, span])
            if mixes:
                queries[2][:, span] = jnp.where(position % 2 == 1, third[:, span], second[:, span])
        refs = (q_ref, second)
        attend(heads, count, lambda i, span: refs[i][:, span], (one, two), (v_one, v_two), acc_in, stat_in, acc_out, stat_out)

    within(position, (1, 2), run)


def far_kernel(heads, distance, last, position_ref, q_ref, acc_in, stat_in, block, vals, acc_out, *stat_out):
    def run(count):
        attend(heads, count, lambda i, span: q_ref[:, span], (block,), (vals,), acc_in, stat_in, acc_out, None if last else stat_out[0])

    within(position_ref[0], (distance,), run)


def whole(shape):
    return pl.BlockSpec(shape, lambda i: (0, 0))


def near_blocks(position, state, one, two, v_one, v_two, heads, chunk, mixes):
    length, width = state[0].shape
    part = pl.BlockSpec((length, width), lambda i: (0, chunk))
    shapes = [jax.ShapeDtypeStruct((length, width), F32), jax.ShapeDtypeStruct((length, 128), F32)]
    shapes += [jax.ShapeDtypeStruct((length, width), F32)] * (3 if mixes else 2)
    shapes += [jax.ShapeDtypeStruct((length, width), BF16)]
    return pl.pallas_call(
        functools.partial(near_kernel, heads, mixes),
        grid=(1,),
        in_specs=[pl.BlockSpec(memory_space=pltpu.SMEM)]
        + [whole(x.shape) for x in state]
        + [whole(one.shape), whole(two.shape), part, part],
        out_specs=[whole(x.shape) for x in shapes],
        out_shape=shapes,
        compiler_params=pltpu.CompilerParams(vmem_limit_bytes=24 * MIB),
        cost_estimate=pl.CostEstimate(
            flops=14 * length * length * width, bytes_accessed=length * width * 30, transcendentals=0
        ),
        name="near_blocks",
    )(position, *state, one, two, v_one, v_two)


def far_block(position, query, acc, stat, block, values, heads, chunk, distance, last):
    length, width = acc.shape
    shapes = [jax.ShapeDtypeStruct((length, width), BF16 if last else F32)]
    shapes += [] if last else [jax.ShapeDtypeStruct((length, 128), F32)]
    operands = (query, acc, stat, block)
    return pl.pallas_call(
        functools.partial(far_kernel, heads, distance, last),
        grid=(1,),
        in_specs=[pl.BlockSpec(memory_space=pltpu.SMEM)]
        + [whole(x.shape) for x in operands]
        + [pl.BlockSpec((length, width), lambda i: (0, chunk))],
        out_specs=[whole(x.shape) for x in shapes],
        out_shape=shapes,
        compiler_params=pltpu.CompilerParams(vmem_limit_bytes=24 * MIB),
        cost_estimate=pl.CostEstimate(
            flops=6 * length * length * width, bytes_accessed=length * width * 20, transcendentals=0
        ),
        name="far_block",
    )(position, *operands, values)


def project_kernel(count, base, *refs):
    rows, weights = refs[:count], refs[count : 2 * count]
    out = refs[-1]
    total = mm(rows[0][...], weights[0][...])
    for i in range(1, count):
        total += mm(rows[i][...], weights[i][...])
    if base:
        total += refs[2 * count][...]
    out[...] = total.astype(out.dtype)


def project(rows, weights, places, base, dtype):
    length, depth = rows[0].shape
    width = weights[0].shape[1]
    whole = pl.BlockSpec((length, width), lambda i: (0, 0))
    extra = [] if base is None else [base]
    return pl.pallas_call(
        functools.partial(project_kernel, len(rows), base is not None),
        grid=(1,),
        in_specs=[pl.BlockSpec(r.shape, lambda i: (0, 0)) for r in rows]
        + [pl.BlockSpec((depth, width), functools.partial(lambda at, i: (at, 0), at)) for at in places]
        + [whole] * len(extra),
        out_specs=whole,
        out_shape=jax.ShapeDtypeStruct((length, width), dtype),
        compiler_params=pltpu.CompilerParams(vmem_limit_bytes=14 * MIB),
        cost_estimate=pl.CostEstimate(
            flops=2 * len(rows) * length * depth * width, bytes_accessed=4 * length * width, transcendentals=0
        ),
        name="project",
    )(*rows, *weights, *extra)


def ring(x, axis, distance):
    n = lax.axis_size(axis)
    return lax.ppermute(x, axis, [(i, (i + distance) % n) for i in range(n)])


def swap(x, axis, bit):
    n = lax.axis_size(axis)
    return lax.ppermute(x, axis, [(i, i ^ bit) for i in range(n)])


def relayed(block, odd):
    two = ring(block, "seq", 2)
    one = swap(jnp.where(odd, two, block), "seq", 1)
    return one, two


def crossed(two, four, odd):
    again = lax.optimization_barrier(two)
    return swap(jnp.where(odd, four, again), "seq", 1)


def layer(queries, keys, values, directions, beta_logit, out_weight):
    length, _ = queries.shape
    groups = lax.axis_size("head")
    heads = HEADS_AT_ONCE
    position = lax.axis_index("seq")
    group = lax.axis_index("head")
    odd = position % 2 == 1
    where = jnp.reshape(position, (1,)).astype(jnp.int32)

    v_one, v_two = relayed(values, odd)
    v_four = ring(v_two, "seq", 2)
    v_three = crossed(v_two, v_four, odd)
    columns = out_weight.shape[1] // groups
    weights = []
    for p in range(groups):
        piece = lax.dynamic_slice_in_dim(out_weight, (group ^ p) * columns, columns, 1)
        weights.append(piece if p == 0 else swap(piece, "head", p))

    parts = []
    locals_ = local_pass(queries, keys, values, directions, beta_logit, heads)
    for c, (packed, *state) in enumerate(locals_):
        one, two = relayed(packed, odd)
        mixes = c == 0
        acc, stat, _, *queries, relay = near_blocks(where, state, one, two, v_one, v_two, heads, c, mixes)
        four = ring(relay, "seq", 2)
        if mixes:
            three = crossed(two[:length], four, odd)
        else:
            three = ring(one[:length], "seq", 2)
        acc, stat = far_block(where, queries[0], acc, stat, four, v_four, heads, c, 4, False)
        (attended,) = far_block(where, queries[-1], acc, stat, three, v_three, heads, c, 3, True)
        spread = [(0, attended)]
        bit = groups // 2
        while bit:
            spread += [(p ^ bit, swap(x, "head", bit)) for p, x in spread]
            bit //= 2
        parts.append([(x, weights[p], c) for p, x in spread])
    late = parts[-1][1::2]
    early = sum(parts[:-1], []) + parts[-1][::2]
    mixed = None
    for group_parts, dtype in ((early, F32), (late, BF16)):
        mixed = project(*zip(*group_parts), mixed, dtype)
    return mixed


def solution(mesh):
    return jax.shard_map(
        layer,
        mesh=mesh,
        in_specs=(
            P("seq", "head"),
            P("seq", "head"),
            P("seq", "head"),
            P("seq", "head"),
            P("head", "seq"),
            P("head", None),
        ),
        out_specs=P("seq", "head"),
        check_vma=False,
    )
```
